128 devices in a mesh: expert: 8 (over y_lo, x), tile: 16 (over z, y_hi, core).
Axes of the slice: x: 4, y: 4 (y_hi: 2, y_lo: 2; y = y_hi * 2 + y_lo), z: 4, core: 2. Of those that a mesh axis runs over, the one named last changes fastest.
Arguments:
- activations: bfloat16 [6144, 6144], P(('expert', 'tile')), may hold values from -40 to 40
- expert_ids: int32 [6144, 2], P(('expert', 'tile')), may hold values from 0 to 7, all different within a row; in each aligned block of 48 rows (0 to 47, 48 to 95, ...) at most 24 rows name the same one
Outputs:
- hessian: float32 [8, 6144, 6144], P('expert', 'tile')
- panels: float32 [8, 6144, 1536], P('expert', 'tile')
The draws below stay inside these ranges and needn't reach their ends.
Inputs may be any that keep to these rules, and one draw needn't show every extreme that they name: `expert_ids`: each row names 2 different experts; within the rows of one device no expert is named more than 24 times, a bound that some block reaches; every expert is named by some row.
All inputs are finite; a program needn't handle non-finite values.
Results may differ from the reference program's by a relative error of at most 0.0003.
Values may be sent and summed in bfloat16 or wider, within the bound.
No kernel may reach another device: no remote copies, remote signals or barrier semaphores. Data moves between devices by JAX's collectives and lax.ppermute only.
A program may use at most 256 MiB of HBM per device.

```python
import math
import jax
import jax.numpy as jnp
import numpy as np
from jax import lax

D = 6144
TOP = 2
EXPERTS = 8
TOK_DEV = 48
PANEL = 768
CAP = 24
TOKENS = 6144


def draw_activations(key, part):
    column_key = jax.random.fold_in(key, 11)
    position = jnp.arange(D, dtype=jnp.float32) / jnp.float32(max(D - 1, 1))
    column_scale = jnp.power(jnp.float32(10.0), 0.5 * position)
    values = jnp.clip(jax.random.normal(column_key, (TOKENS, D), jnp.float32), -6.0, 6.0)
    return (values * column_scale[None, :]).astype(jnp.bfloat16)


def assign_block(key, own, number, rows, amount, top, most, lean):
    sequence = jax.random.permutation(key, amount)
    heavy_load, common = load_shares(amount, rows * top, most, lean, True), load_shares(amount, rows * top, most, lean, False)
    places = jnp.arange(amount)

    def named(tallies, offset_by):
        used = int((tallies > 0).sum())
        fixed = max(1, used // 4)
        passed = fixed + (places - fixed + offset_by * (used - fixed)) % max(1, amount - fixed)
        return jnp.zeros((amount,), jnp.int32).at[sequence[jnp.where(places < fixed, places, passed)]].set(jnp.asarray(tallies, jnp.int32))

    tallies = jnp.where(number % 4 == 0, named(heavy_load, number // 4), named(common, number - number // 4 - 1))
    mixed = jax.random.permutation(jax.random.fold_in(own, 3), amount)
    giver, receiver = mixed[0:amount // 2 * 2:2], mixed[1:amount // 2 * 2:2]
    room = jnp.minimum(tallies[giver] - 1, most - tallies[receiver]) // 2
    room = jnp.where((giver == sequence[0]) | (receiver == sequence[0]) | (tallies[receiver] == 0), 0, jnp.maximum(room, 0))
    passed = jax.random.randint(jax.random.fold_in(own, 4), (amount // 2,), 0, 1 << 20) % (room + 1)
    tallies = tallies.at[giver].add(-passed).at[receiver].add(passed)
    labels = jnp.searchsorted(jnp.cumsum(tallies), jnp.arange(rows * top), side="right").astype(jnp.int32)
    grid = labels.reshape(top, rows).T
    grid = grid[jax.random.permutation(jax.random.fold_in(own, 1), rows)]
    offset_by = jax.random.randint(jax.random.fold_in(own, 2), (rows, 1), 0, top)
    return jnp.take_along_axis(grid, (jnp.arange(top)[None, :] + offset_by) % top, axis=1)


def load_shares(count, total, limit, lean, full):
    loads = [(1 << 20) // math.isqrt(grade ** lean) + 1 for grade in range(1, count + 1)]
    largest = limit if full else min(limit, max(-(-total // count), total * loads[0] // sum(loads)))
    least = 1 if total - largest >= count - 1 else 0
    given, rest = [largest] + [least] * (count - 1), total - largest - least * (count - 1)
    while rest > 0:
        candidates = [i for i in range(1, count) if given[i] < largest] or [i for i in range(1, count) if given[i] < limit]
        pool, remaining = sum([loads[i] for i in candidates]), rest
        for i in candidates:
            extra = min(limit - given[i], max(1, remaining * loads[i] // pool), rest)
            given[i] = given[i] + extra
            rest = rest - extra
    return np.array(given)


def setup_inputs(seed: int = 0) -> dict:
    splits = jax.random.split(jax.random.key(seed), 3)
    activations = draw_activations(jax.random.fold_in(splits[2], 71), 0)
    expert_ids_keys = jax.random.split(jax.random.fold_in(splits[1], 1), TOKENS // TOK_DEV)
    expert_ids_turns = jax.random.permutation(jax.random.fold_in(splits[1], 3), TOKENS // TOK_DEV)
    expert_ids = jax.vmap(lambda own, number: assign_block(jax.random.fold_in(splits[1], 2), own, number, TOK_DEV, EXPERTS, TOP, CAP, 2))(expert_ids_keys, expert_ids_turns).reshape((TOKENS, TOP))
    return dict(activations=activations, expert_ids=expert_ids)


damp_fraction = 0.01

def factor_panels(hessian):
    row_index = jnp.arange(D, dtype=jnp.int32)
    factors = []
    for panel in range(2):
        panel_start = panel * PANEL
        panel_block = hessian[:, panel_start:panel_start + PANEL]
        for earlier in factors:
            panel_block = panel_block - jnp.dot(earlier, earlier[panel_start:panel_start + PANEL].T, precision=lax.Precision.HIGHEST)
        diagonal_factor = jnp.linalg.cholesky(panel_block[panel_start:panel_start + PANEL])
        panel_factor = jax.scipy.linalg.solve_triangular(diagonal_factor, panel_block.T, lower=True).T
        column_index = panel_start + jnp.arange(PANEL, dtype=jnp.int32)
        lower_mask = row_index[:, None] >= column_index[None, :]
        factors.append(jnp.where(lower_mask, panel_factor, jnp.float32(0.0)))
    return jnp.concatenate(factors, axis=1)

def reference(activations, expert_ids):
    features = activations.astype(jnp.float32)
    expert_iota = jnp.arange(EXPERTS, dtype=jnp.int32)
    routed = jnp.sum((expert_ids[:, :, None] == expert_iota[None, None, :]).astype(jnp.float32), axis=1)
    counts = jnp.sum(routed, axis=0)
    identity = jnp.eye(D, dtype=jnp.float32)

    def one_expert(inputs):
        token_weight, expert_count = inputs
        gram_sum = jnp.dot((features * token_weight[:, None]).T, features, precision=lax.Precision.HIGHEST)
        hessian = gram_sum * (2.0 / expert_count)
        damping = damp_fraction * jnp.trace(hessian) / D
        hessian = hessian + damping * identity
        return (hessian, factor_panels(hessian))
    hessian, panels = lax.map(one_expert, (routed.T, counts))
    return (hessian, panels)
```

```python
import jax
import jax.numpy as jnp
from jax import lax
from jax.experimental import pallas as pl
from jax.experimental.pallas import tpu as pltpu
from jax.sharding import PartitionSpec as P

PANEL = 768
LEAD = 2 * PANEL
EXTRA = 128
BLOCK = 256
HALF = 128
MICRO = 8
DAMP = 0.01

f32 = jnp.float32
bf16 = jnp.bfloat16


def lane_fill(column):
    return jnp.broadcast_to(column, (column.shape[0], HALF))


def row_fill(block, i):
    return jnp.broadcast_to(block[i : i + 1, :], block.shape)


def tree_sum(terms):
    terms = list(terms)
    while len(terms) > 1:
        terms = [
            terms[i] + terms[i + 1] if i + 1 < len(terms) else terms[i]
            for i in range(0, len(terms), 2)
        ]
    return terms[0]


def inverse_factor(read, write):
    groups = HALF // MICRO
    sub = lax.broadcasted_iota(jnp.int32, (MICRO, HALF), 0)
    lane = lax.broadcasted_iota(jnp.int32, (MICRO, HALF), 1)
    a = [read(g) for g in range(groups)]
    e = [(lane == sub + MICRO * g).astype(f32) for g in range(groups)]
    for g in range(groups):
        first = MICRO * g
        cols = [lane_fill(a[g][:, first + c : first + c + 1]) for c in range(MICRO)]
        forward, full_a, full_e = e[g], a[g], e[g]
        pivots = None
        for i in range(MICRO):
            r = 1.0 / row_fill(cols[i], i)
            pivots = r if pivots is None else jnp.where(sub >= i, r, pivots)
            scaled = cols[i] * r
            both = jnp.where(sub == i, 1.0 - r, scaled)
            below = jnp.where(sub > i, scaled, 0.0)
            for c in range(i + 1, MICRO):
                cols[c] = cols[c] - both * row_fill(cols[c], i)
            forward = forward - below * row_fill(forward, i)
            full_a = full_a - both * row_fill(full_a, i)
            full_e = full_e - both * row_fill(full_e, i)
        write(g, forward * jnp.sqrt(pivots))
        if g + 1 == groups:
            break
        rows_a = [row_fill(full_a, i) for i in range(MICRO)]
        rows_e = [row_fill(full_e, i) for i in range(MICRO)]
        for q in range(g + 1, groups):
            coef = [lane_fill(a[q][:, first + i : first + i + 1]) for i in range(MICRO)]
            a[q] = a[q] - tree_sum([coef[i] * rows_a[i] for i in range(MICRO)])
            e[q] = e[q] - tree_sum([coef[i] * rows_e[i] for i in range(MICRO)])


def split(x):
    hi = x.astype(bf16)
    return hi, (x - hi.astype(f32)).astype(bf16)


def dot_t(a, b):
    return lax.dot_general(a, b, (((1,), (1,)), ((), ())), preferred_element_type=f32)


def dot3(a, b):
    return dot_t(a[0], b[0]) + (dot_t(a[0], b[1]) + dot_t(a[1], b[0]))


def exact_t(a, b):
    return lax.dot_general(
        a, b, (((1,), (1,)), ((), ())), precision=lax.Precision.HIGHEST, preferred_element_type=f32
    )


def exact(a, b):
    return jnp.dot(a, b, precision=lax.Precision.HIGHEST, preferred_element_type=f32)


def blk(i):
    return pl.ds(pl.multiple_of(i * BLOCK, BLOCK), BLOCK)


def cholesky_kernel(scalars, gram, lh, lm, wh, wm, col, dd, wd, lower):
    count = LEAD // BLOCK
    scale = scalars[0]
    damping = scalars[1]
    eye = (
        lax.broadcasted_iota(jnp.int32, (BLOCK, BLOCK), 0)
        == lax.broadcasted_iota(jnp.int32, (BLOCK, BLOCK), 1)
    ).astype(f32)

    @pl.loop(0, count)
    def _(j):
        @pl.loop(j, count)
        def _(i):
            col[blk(i), :] = gram[blk(i), blk(j)] * scale

            @pl.loop(0, j)
            def _(k):
                col[blk(i), :] -= dot3(
                    (lh[blk(i), blk(k)], lm[blk(i), blk(k)]),
                    (lh[blk(j), blk(k)], lm[blk(j), blk(k)]),
                )

        diag = col[blk(j), :] + damping * eye
        dd[0] = diag[:HALF, :HALF]
        dd[1] = diag[HALF:, HALF:]
        lower[...] = diag[HALF:, :HALF]

        @pl.loop(0, 2)
        def _(s):
            def write(g, value):
                wd[s, g * MICRO : (g + 1) * MICRO, :] = value

            inverse_factor(lambda g: dd[s, g * MICRO : (g + 1) * MICRO, :], write)

            @pl.when(s == 0)
            def _():
                lower[...] = exact_t(lower[...], wd[0])
                dd[1] = dd[1] - exact_t(lower[...], lower[...])

        corner = -exact(wd[1], exact(lower[...], wd[0]))
        for piece, value in (
            ((slice(0, HALF), slice(0, HALF)), wd[0]),
            ((slice(HALF, BLOCK), slice(0, HALF)), corner),
            ((slice(HALF, BLOCK), slice(HALF, BLOCK)), wd[1]),
            ((slice(0, HALF), slice(HALF, BLOCK)), jnp.zeros((HALF, HALF), f32)),
        ):
            hi, mid = split(value)
            wh[(j, *piece)] = hi
            wm[(j, *piece)] = mid

        @pl.loop(j + 1, count)
        def _(i):
            hi, mid = split(dot3(split(col[blk(i), :]), (wh[j], wm[j])))
            lh[blk(i), blk(j)] = hi
            lm[blk(i), blk(j)] = mid


def cholesky_lead(gram, scalars):
    count = LEAD // BLOCK
    vmem = pl.BlockSpec(memory_space=pltpu.VMEM)
    return pl.pallas_call(
        cholesky_kernel,
        out_shape=(
            jax.ShapeDtypeStruct((LEAD, LEAD), bf16),
            jax.ShapeDtypeStruct((LEAD, LEAD), bf16),
            jax.ShapeDtypeStruct((count, BLOCK, BLOCK), bf16),
            jax.ShapeDtypeStruct((count, BLOCK, BLOCK), bf16),
        ),
        in_specs=[pl.BlockSpec(memory_space=pltpu.SMEM), vmem],
        out_specs=(vmem,) * 4,
        scratch_shapes=[
            pltpu.VMEM((LEAD, BLOCK), f32),
            pltpu.VMEM((2, HALF, HALF), f32),
            pltpu.VMEM((2, HALF, HALF), f32),
            pltpu.VMEM((HALF, HALF), f32),
        ],
        compiler_params=pltpu.CompilerParams(vmem_limit_bytes=40 << 20),
        cost_estimate=pl.CostEstimate(
            flops=150_000_000_000, bytes_accessed=30_000_000, transcendentals=0
        ),
        name="cholesky_lead",
    )(scalars, gram)


def solve_kernel(first_row, rows, lh, lm, wh, wm, out, fh, fm):
    count = LEAD // BLOCK
    rows_device = rows.shape[0]
    row = first_row[0] + lax.broadcasted_iota(jnp.int32, (rows_device, BLOCK), 0)
    lane = lax.broadcasted_iota(jnp.int32, (rows_device, BLOCK), 1)
    for j in range(count):
        here = slice(j * BLOCK, (j + 1) * BLOCK)
        value = rows[:, here]
        for k in range(j):
            there = slice(k * BLOCK, (k + 1) * BLOCK)
            value = value - dot3((fh[:, there], fm[:, there]), (lh[here, there], lm[here, there]))
        value = dot3(split(value), (wh[j], wm[j]))
        hi, mid = split(value)
        fh[:, here] = hi
        fm[:, here] = mid
        out[:, here] = jnp.where(row >= lane + j * BLOCK, value, 0.0)


def solve_own(rows, factors, first_row):
    vmem = pl.BlockSpec(memory_space=pltpu.VMEM)
    return pl.pallas_call(
        solve_kernel,
        out_shape=jax.ShapeDtypeStruct(rows.shape, f32),
        in_specs=[pl.BlockSpec(memory_space=pltpu.SMEM)] + [vmem] * 5,
        out_specs=vmem,
        scratch_shapes=[pltpu.VMEM(rows.shape, bf16), pltpu.VMEM(rows.shape, bf16)],
        compiler_params=pltpu.CompilerParams(vmem_limit_bytes=40 << 20),
        cost_estimate=pl.CostEstimate(
            flops=10_000_000_000, bytes_accessed=20_000_000, transcendentals=0
        ),
        name="solve_own",
    )(first_row.reshape(1), rows, *factors)


def gram_of(left, right):
    return jnp.einsum("tr,tc->rc", left, right, preferred_element_type=f32)


def local(activations, expert_ids):
    tile_count = lax.axis_size("tile")
    group_count = lax.axis_size("expert")
    token_count, width = activations.shape
    capacity = 2 * token_count * expert_ids.shape[1] // group_count
    rows_device = width // tile_count
    tile_index = lax.axis_index("tile")
    first_row = tile_index * rows_device

    experts = jnp.arange(group_count, dtype=jnp.int32)
    routed = jnp.sum((expert_ids[..., None] == experts).astype(jnp.int32), axis=1)
    before = (
        jnp.arange(token_count)[:, None] > jnp.arange(token_count)[None, :]
    ).astype(bf16)
    slot = jnp.dot(before, routed.astype(bf16), preferred_element_type=f32).astype(jnp.int32)
    slots = jnp.arange(capacity, dtype=jnp.int32)
    selector = (routed[..., None] > 0) & (slot[..., None] == slots)
    selector = selector.reshape(token_count, group_count * capacity).astype(bf16)

    squares = jnp.sum(jnp.square(activations.astype(f32)), axis=1, keepdims=True)
    sq_hi, sq_rest = squares.astype(bf16), squares
    pieces = [jnp.ones((token_count, 1), bf16)]
    for _ in range(3):
        piece = sq_rest.astype(bf16)
        pieces.append(piece)
        sq_rest = sq_rest - piece.astype(f32)
    extra = jnp.concatenate(
        pieces + [jnp.zeros((token_count, EXTRA - len(pieces)), bf16)], axis=1
    )
    head = jnp.concatenate([activations[:, :LEAD], extra], axis=1)
    tail = activations[:, LEAD:]

    def dispatch(x):
        packed = lax.dot_general(
            selector, x, (((0,), (0,)), ((), ())), preferred_element_type=f32
        ).astype(bf16)
        packed = packed.reshape(group_count, capacity, x.shape[1])
        out = lax.all_to_all(packed, "expert", split_axis=0, concat_axis=0, tiled=True)
        return out.reshape(group_count * capacity, x.shape[1])

    got_head = dispatch(head)
    all_head = lax.all_gather(got_head, "tile", axis=0, tiled=True)
    got_tail = dispatch(tail)
    all_tail = lax.all_gather(got_tail, "tile", axis=0, tiled=True)

    sums = jnp.sum(all_head[:, LEAD : LEAD + 4].astype(f32), axis=0)
    scale = 2.0 / sums[0]
    damping = DAMP * ((sums[1] + (sums[2] + sums[3])) * scale) / width

    lead = all_head[:, :LEAD]
    gram = jnp.concatenate(
        [
            gram_of(lead, lead[:, :PANEL]),
            jnp.pad(gram_of(lead[:, PANEL:], lead[:, PANEL:]), ((PANEL, 0), (0, 0))),
        ],
        axis=1,
    )
    factors = cholesky_lead(gram, jnp.stack([scale, damping]))

    own = jnp.where(
        first_row < LEAD,
        lax.dynamic_slice_in_dim(lead, jnp.minimum(first_row, LEAD - rows_device), rows_device, 1),
        lax.dynamic_slice_in_dim(
            all_tail, jnp.maximum(first_row - LEAD, 0), rows_device, 1
        ),
    )
    rows = first_row + jnp.arange(rows_device, dtype=jnp.int32)
    hessian = []
    for part, start in ((lead, 0), (all_tail, LEAD)):
        columns = start + jnp.arange(part.shape[1], dtype=jnp.int32)
        hessian.append(
            gram_of(own, part) * scale
            + jnp.where(rows[:, None] == columns[None, :], damping, jnp.float32(0.0))
        )
    panels = solve_own(hessian[0], factors, first_row)
    return (jnp.concatenate(hessian, axis=1)[None], panels[None])


def solution(mesh):
    placed = (P(("expert", "tile"), None), P(("expert", "tile"), None))
    return jax.shard_map(
        local,
        mesh=mesh,
        in_specs=placed,
        out_specs=(P("expert", "tile", None), P("expert", "tile", None)),
        check_vma=False,
    )
```

```python
import functools

import jax
import jax.numpy as jnp
from jax import lax
from jax.experimental import pallas as pl
from jax.experimental.pallas import tpu as pltpu
from jax.sharding import PartitionSpec as P

PANEL = 768
LEAD = 2 * PANEL
EXTRA = 128
BLOCK = 256
HALF = 128
MICRO = 8
STRIP = 64
DAMP = 0.01
TILE = 512
WIDTH = 6144

f32 = jnp.float32
bf16 = jnp.bfloat16


def lane_fill(column):
    return jnp.broadcast_to(column, (column.shape[0], HALF))


def row_fill(block, i):
    return jnp.broadcast_to(block[i : i + 1, :], block.shape)


def tree_sum(terms):
    terms = list(terms)
    while len(terms) > 1:
        terms = [
            terms[i] + terms[i + 1] if i + 1 < len(terms) else terms[i]
            for i in range(0, len(terms), 2)
        ]
    return terms[0]


def eliminate(cols, ahead, forward, full_a, full_e, sub):
    roots = None
    for i in range(0, MICRO, 2):
        u, v = cols[i], cols[i + 1]
        p, q, s = row_fill(u, i), row_fill(u, i + 1), row_fill(v, i + 1)
        rd = 1.0 / (p * s - q * q)
        rp = 1.0 / p
        alpha = jnp.where(sub == i + 1, q, u * s - v * q)
        alpha = jnp.where(sub == i, -s, alpha) * rd
        beta = jnp.where(sub == i, q, v * p - u * q)
        beta = jnp.where(sub == i + 1, -p, beta) * rd
        alpha = jnp.where(sub == i, 1.0 + alpha, alpha)
        beta = jnp.where(sub == i + 1, 1.0 + beta, beta)
        below_a = jnp.where(sub > i + 1, alpha, jnp.where(sub == i + 1, q * rp, 0.0))
        below_b = jnp.where(sub > i + 1, beta, 0.0)

        def up(x):
            return x - (alpha * row_fill(x, i) + beta * row_fill(x, i + 1))

        cols = [x if c < i + 2 else up(x) for c, x in enumerate(cols)]
        ahead = [up(x) for x in ahead]
        forward = forward - (below_a * row_fill(forward, i) + below_b * row_fill(forward, i + 1))
        full_a, full_e = up(full_a), up(full_e)
        pair = jnp.where(sub == i, rp, p * rd)
        roots = pair if roots is None else jnp.where(sub >= i, pair, roots)
    return ahead, forward * jnp.sqrt(roots), full_a, full_e


def inverse_factor(read, write, rest_a, rest_e):
    sub = lax.broadcasted_iota(jnp.int32, (MICRO, HALF), 0)
    lane = lax.broadcasted_iota(jnp.int32, (MICRO, HALF), 1)
    unit = lambda g: (lane == sub + MICRO * g).astype(f32)
    groups, width = HALF // MICRO, STRIP // MICRO

    def filled(x, first):
        return [lane_fill(x[:, first + c : first + c + 1]) for c in range(MICRO)]

    for base in range(0, HALF, STRIP):
        final = base + STRIP == HALF
        at = [slice(base + MICRO * g, base + MICRO * (g + 1)) for g in range(width)]
        a = [read(g) if base == 0 else rest_a[at[g], :] for g in range(width)]
        e = [unit(g) if base == 0 else rest_e[at[g], :] for g in range(width)]
        cols = filled(a[0], base)
        for g in range(width):
            first = base + MICRO * g
            more = g + 1 < width
            others = [q for q in range(width) if q != g and not (final and q < g)]
            coef = {q: filled(a[q], first) for q in others}
            ahead = filled(a[g], first + MICRO) if more else []
            following = filled(a[g + 1], first + MICRO) if more else []
            ahead, w, full_a, full_e = eliminate(cols, ahead, e[g], a[g], e[g], sub)
            write(base // MICRO + g, w)
            if more:
                cols = [
                    x - tree_sum([coef[g + 1][i] * row_fill(y, i) for i in range(MICRO)])
                    for x, y in zip(following, ahead)
                ]
            rows_a = [row_fill(full_a, i) for i in range(MICRO)]
            rows_e = [row_fill(full_e, i) for i in range(MICRO)]
            a[g], e[g] = full_a, full_e
            for q in others:
                a[q] = a[q] - tree_sum([coef[q][i] * rows_a[i] for i in range(MICRO)])
                e[q] = e[q] - tree_sum([coef[q][i] * rows_e[i] for i in range(MICRO)])
        if final:
            break
        pad = lambda rows: jnp.concatenate(
            ([jnp.zeros((base, HALF), f32)] if base else [])
            + rows
            + [jnp.zeros((HALF - base - STRIP, HALF), f32)],
            axis=0,
        )
        below = slice(base + STRIP, HALF)
        if base == 0:
            old_a = jnp.concatenate([read(g) for g in range(width, groups)], axis=0)
            old_e = jnp.concatenate([unit(g) for g in range(width, groups)], axis=0)
        else:
            old_a, old_e = rest_a[below, :], rest_e[below, :]
        update = exact(old_a, jnp.concatenate([pad(a), pad(e)], axis=1))
        rest_a[below, :] = old_a - update[:, :HALF]
        rest_e[below, :] = old_e - update[:, HALF:]


def split(x):
    hi = x.astype(bf16)
    return hi, (x - hi.astype(f32)).astype(bf16)


def dot_t(a, b):
    return lax.dot_general(a, b, (((1,), (1,)), ((), ())), preferred_element_type=f32)


def dot3(a, b):
    return dot_t(a[0], b[0]) + (dot_t(a[0], b[1]) + dot_t(a[1], b[0]))


def exact_t(a, b):
    return lax.dot_general(
        a, b, (((1,), (1,)), ((), ())), precision=lax.Precision.HIGHEST, preferred_element_type=f32
    )


def exact(a, b):
    return jnp.dot(a, b, precision=lax.Precision.HIGHEST, preferred_element_type=f32)


def blk(i):
    return pl.ds(pl.multiple_of(i * BLOCK, BLOCK), BLOCK)


def offsets(arrays):
    starts = [0]
    for a in arrays:
        starts.append(starts[-1] + a.shape[0])
    return starts


def gather_columns(pieces, columns, target, sem):
    starts = offsets(pieces)
    copies = [
        pltpu.make_async_copy(
            piece.at[:, columns], target.at[pl.ds(first, piece.shape[0])], sem.at[n]
        )
        for n, (piece, first) in enumerate(zip(pieces, starts))
    ]
    return copies


def cross(a, b):
    return lax.dot_general(a, b, (((0,), (0,)), ((), ())), preferred_element_type=f32)


def panel_kernel(panel, pieces_count, *refs):
    count = PANEL // BLOCK
    pieces = refs[:pieces_count]
    refs = refs[pieces_count:]
    if panel == 0:
        stats, lh, lm, wh, wm, x, sem, col, dd, wd, lower, ra, re = refs
    else:
        stats, eh_all, em_all, lh, lm, wh, wm, x, sem, col, dd, wd, lower, ra, re, eh, em = refs
    first = panel * PANEL
    rows_count = (LEAD - first) // BLOCK
    columns = pl.ds(first, x.shape[1])
    copies = gather_columns(pieces, columns, x, sem)
    if panel == 1:
        below = pl.ds(PANEL, PANEL)
        copies.append(pltpu.make_async_copy(eh_all.at[below], eh, sem.at[len(copies)]))
        copies.append(pltpu.make_async_copy(em_all.at[below], em, sem.at[len(copies)]))
    for c in copies:
        c.start()
    for c in copies:
        c.wait()
    if panel == 0:
        sums = jnp.sum(x[:, LEAD:].astype(f32), axis=0, keepdims=True)
        scale = 2.0 / sums[:, 0:1]
        trace = (sums[:, 1:2] + (sums[:, 2:3] + sums[:, 3:4])) * scale
        damping = DAMP * trace / WIDTH
        stats[0:1, :] = jnp.broadcast_to(scale, (1, EXTRA))
        stats[1:2, :] = jnp.broadcast_to(damping, (1, EXTRA))
        stats[2:8, :] = jnp.zeros((6, EXTRA), f32)
    scale = stats[0:1, 0:1]
    damping = stats[1:2, 0:1]
    eye = (
        lax.broadcasted_iota(jnp.int32, (BLOCK, BLOCK), 0)
        == lax.broadcasted_iota(jnp.int32, (BLOCK, BLOCK), 1)
    ).astype(f32)

    @pl.loop(0, count)
    def _(j):
        @pl.loop(j, rows_count)
        def _(i):
            value = cross(x[:, blk(i)], x[:, blk(j)]) * scale
            if panel == 1:
                value = value - dot3((eh[blk(i), :], em[blk(i), :]), (eh[blk(j), :], em[blk(j), :]))
            col[blk(i), :] = value

            @pl.loop(0, j)
            def _(k):
                col[blk(i), :] -= dot3(
                    (lh[blk(i), blk(k)], lm[blk(i), blk(k)]),
                    (lh[blk(j), blk(k)], lm[blk(j), blk(k)]),
                )

        diag = col[blk(j), :] + damping * eye
        dd[0] = diag[:HALF, :HALF]
        dd[1] = diag[HALF:, HALF:]
        lower[...] = diag[HALF:, :HALF]

        @pl.loop(0, 2)
        def _(s):
            def write(g, value):
                wd[s, g * MICRO : (g + 1) * MICRO, :] = value

            inverse_factor(lambda g: dd[s, g * MICRO : (g + 1) * MICRO, :], write, ra, re)

            @pl.when(s == 0)
            def _():
                lower[...] = exact_t(lower[...], wd[0])
                dd[1] = dd[1] - exact_t(lower[...], lower[...])

        corner = -exact(wd[1], exact(lower[...], wd[0]))
        for piece, value in (
            ((slice(0, HALF), slice(0, HALF)), wd[0]),
            ((slice(HALF, BLOCK), slice(0, HALF)), corner),
            ((slice(HALF, BLOCK), slice(HALF, BLOCK)), wd[1]),
            ((slice(0, HALF), slice(HALF, BLOCK)), jnp.zeros((HALF, HALF), f32)),
        ):
            hi, mid = split(value)
            wh[(j, *piece)] = hi
            wm[(j, *piece)] = mid

        @pl.loop(j + 1, rows_count)
        def _(i):
            hi, mid = split(dot3(split(col[blk(i), :]), (wh[j], wm[j])))
            lh[blk(i), blk(j)] = hi
            lm[blk(i), blk(j)] = mid


def factor_panel(panel, pieces, stats=None, earlier=None):
    rows = LEAD - panel * PANEL
    tokens = sum(p.shape[0] for p in pieces)
    vmem = pl.BlockSpec(memory_space=pltpu.VMEM)
    count = PANEL // BLOCK
    factor = jax.ShapeDtypeStruct((rows, PANEL), bf16)
    inverse = jax.ShapeDtypeStruct((count, BLOCK, BLOCK), bf16)
    out_shape = (factor, factor, inverse, inverse)
    if panel == 0:
        out_shape = (jax.ShapeDtypeStruct((8, EXTRA), f32),) + out_shape
        extra, extra_specs = (), []
    else:
        extra = (stats, *earlier)
        hbm = pl.BlockSpec(memory_space=pl.ANY)
        extra_specs = [vmem, hbm, hbm]
    return pl.pallas_call(
        functools.partial(panel_kernel, panel, len(pieces)),
        out_shape=out_shape,
        in_specs=[pl.BlockSpec(memory_space=pl.ANY)] * len(pieces) + extra_specs,
        out_specs=(vmem,) * len(out_shape),
        scratch_shapes=[
            pltpu.VMEM((tokens, LEAD + EXTRA if panel == 0 else PANEL), bf16),
            pltpu.SemaphoreType.DMA((len(pieces) + 2,)),
            pltpu.VMEM((rows, BLOCK), f32),
            pltpu.VMEM((2, HALF, HALF), f32),
            pltpu.VMEM((2, HALF, HALF), f32),
            pltpu.VMEM((HALF, HALF), f32),
            pltpu.VMEM((HALF, HALF), f32),
            pltpu.VMEM((HALF, HALF), f32),
        ]
        + [pltpu.VMEM((PANEL, PANEL), bf16)] * (2 * panel),
        compiler_params=pltpu.CompilerParams(vmem_limit_bytes=60 << 20),
        cost_estimate=pl.CostEstimate(
            flops=40_000_000_000, bytes_accessed=20_000_000, transcendentals=0
        ),
        name="factor_panel" + str(panel),
    )(*pieces, *extra)


def own_kernel(n, final, first_row, *refs):
    lead, tail = refs[:n], refs[n : 2 * n]
    refs = refs[2 * n :]
    if final:
        (partial, stats, lh0, lm0, wh0, wm0, lh1, lm1, wh1, wm1) = refs[:10]
        hessian, panels, own, own_sem, x, x_sem, h, h_sem, p, p_sem, fh, fm, rows = refs[10:]
        scale = stats[0:1, 0:1]
        damping = stats[1:2, 0:1]
    else:
        hessian, own, own_sem, x, x_sem, h, h_sem = refs
    rows_device = own.shape[1]
    tiles = WIDTH // TILE
    lead_tiles = LEAD // TILE
    start = pl.multiple_of(first_row[0], HALF)

    def fetch(c, slot, act):
        @pl.when(c < lead_tiles)
        def _():
            at = pl.multiple_of(c * TILE, TILE)
            for copy in gather_columns(lead, pl.ds(at, TILE), x.at[slot], x_sem.at[slot]):
                act(copy)

        @pl.when(jnp.logical_and(c >= lead_tiles, c < tiles))
        def _():
            at = pl.multiple_of((c - lead_tiles) * TILE, TILE)
            for copy in gather_columns(tail, pl.ds(at, TILE), x.at[slot], x_sem.at[slot]):
                act(copy)

        if final:

            @pl.when(c < tiles)
            def _():
                at = pl.multiple_of(c * TILE, TILE)
                act(pltpu.make_async_copy(partial.at[:, pl.ds(at, TILE)], p.at[slot], p_sem.at[slot]))

    def take_own(act):
        @pl.when(start < LEAD)
        def _():
            at = pl.multiple_of(start, HALF)
            for copy in gather_columns(lead, pl.ds(at, rows_device), own, own_sem):
                act(copy)

        @pl.when(start >= LEAD)
        def _():
            at = pl.multiple_of(start - LEAD, HALF)
            for copy in gather_columns(tail, pl.ds(at, rows_device), own, own_sem):
                act(copy)

    begin = lambda copy: copy.start()
    finish = lambda copy: copy.wait()
    take_own(begin)
    fetch(0, 0, begin)
    take_own(finish)
    row = start + lax.broadcasted_iota(jnp.int32, (rows_device, TILE), 0)
    lane = lax.broadcasted_iota(jnp.int32, (rows_device, TILE), 1)

    def out_copy(c, slot):
        at = pl.multiple_of(c * TILE, TILE)
        return pltpu.make_async_copy(h.at[slot], hessian.at[:, pl.ds(at, TILE)], h_sem.at[slot])

    def tile(c, keep):
        slot = lax.rem(c, 2)
        fetch(c + 1, 1 - slot, begin)
        fetch(c, slot, finish)
        value = cross(own[...], x[slot])
        if final:
            value = (value + p[slot]) * scale
            value = value + jnp.where(row == lane + c * TILE, damping, 0.0)

        @pl.when(c >= 2)
        def _():
            out_copy(c - 2, slot).wait()

        h[slot] = value
        if keep:
            rows[:, pl.ds(pl.multiple_of(c * TILE, TILE), TILE)] = value
        out_copy(c, slot).start()

    @pl.loop(0, lead_tiles if final else tiles)
    def _(c):
        tile(c, final)

    if final:
        brow = start + lax.broadcasted_iota(jnp.int32, (rows_device, BLOCK), 0)
        blane = lax.broadcasted_iota(jnp.int32, (rows_device, BLOCK), 1)
        half = PANEL // BLOCK
        for j in range(2 * half):
            here = slice(j * BLOCK, (j + 1) * BLOCK)
            value = rows[:, here]
            for k in range(j):
                there = slice(k * BLOCK, (k + 1) * BLOCK)
                if k < half:
                    rhs = (lh0[here, there], lm0[here, there])
                else:
                    a = slice((j - half) * BLOCK, (j - half + 1) * BLOCK)
                    b = slice((k - half) * BLOCK, (k - half + 1) * BLOCK)
                    rhs = (lh1[a, b], lm1[a, b])
                value = value - dot3((fh[:, there], fm[:, there]), rhs)
            w = (wh0[j], wm0[j]) if j < half else (wh1[j - half], wm1[j - half])
            value = dot3(split(value), w)
            hi, mid = split(value)
            fh[:, here] = hi
            fm[:, here] = mid
            panels[:, here] = jnp.where(brow >= blane + j * BLOCK, value, 0.0)

        @pl.loop(lead_tiles, tiles)
        def _(c):
            tile(c, False)

    out_copy(tiles - 2, (tiles - 2) % 2).wait()
    out_copy(tiles - 1, (tiles - 1) % 2).wait()


def own_rows(first_row, lead, tail, rows_device, rest=None):
    tokens = sum(p.shape[0] for p in lead)
    n = len(lead)
    final = rest is not None
    vmem = pl.BlockSpec(memory_space=pltpu.VMEM)
    hbm = pl.BlockSpec(memory_space=pl.ANY)
    block = jax.ShapeDtypeStruct((rows_device, WIDTH), f32)
    scratch = [
        pltpu.VMEM((tokens, rows_device), bf16),
        pltpu.SemaphoreType.DMA((n,)),
        pltpu.VMEM((2, tokens, TILE), bf16),
        pltpu.SemaphoreType.DMA((2, n)),
        pltpu.VMEM((2, rows_device, TILE), f32),
        pltpu.SemaphoreType.DMA((2,)),
    ]
    if final:
        scratch += [
            pltpu.VMEM((2, rows_device, TILE), f32),
            pltpu.SemaphoreType.DMA((2,)),
            pltpu.VMEM((rows_device, LEAD), bf16),
            pltpu.VMEM((rows_device, LEAD), bf16),
            pltpu.VMEM((rows_device, LEAD), f32),
        ]
    specs = [pl.BlockSpec(memory_space=pltpu.SMEM)] + [hbm] * (2 * n)
    return pl.pallas_call(
        functools.partial(own_kernel, n, final),
        out_shape=(block, jax.ShapeDtypeStruct((rows_device, LEAD), f32)) if final else block,
        in_specs=specs + ([hbm] + [vmem] * 9 if final else []),
        out_specs=(hbm, vmem) if final else hbm,
        scratch_shapes=scratch,
        compiler_params=pltpu.CompilerParams(vmem_limit_bytes=60 << 20),
        cost_estimate=pl.CostEstimate(
            flops=2 * tokens * rows_device * WIDTH, bytes_accessed=40_000_000, transcendentals=0
        ),
        name="own_rows" + str(int(final)),
    )(first_row.reshape(1), *lead, *tail, *(rest or ()))


UP = [(i, (i + 4) % 16) for i in range(16)]
DOWN = [(i, (i + 12) % 16) for i in range(16)]
ACROSS = [(i, i ^ 2) for i in range(16)]
CORE = [(i, i ^ 1) for i in range(16)]


def move(x, pairs):
    return lax.ppermute(x, "tile", pairs)


def both(blocks):
    return [(b, move(b, CORE)) for b in blocks]


def round_one(b):
    return move(b, UP), move(b, DOWN), move(b, ACROSS)


def round_two(up, down, across):
    return move(up, UP), move(across, DOWN), move(up, ACROSS)


def round_three(up_up, down_across, up_across):
    third = up_up.shape[0] // 3
    return (
        move(up_across[:third], UP),
        move(down_across[third : 2 * third], DOWN),
        move(up_up[2 * third :], ACROSS),
    )


def lay_out(pairs):
    return [a for a, _ in pairs] + [b for _, b in pairs]


def local(activations, expert_ids):
    tile_count = lax.axis_size("tile")
    group_count = lax.axis_size("expert")
    token_count, width = activations.shape
    capacity = 2 * token_count * expert_ids.shape[1] // group_count
    rows_device = width // tile_count
    first_row = lax.axis_index("tile") * rows_device

    experts = jnp.arange(group_count, dtype=jnp.int32)
    slots = jnp.arange(capacity, dtype=jnp.int32)
    tokens = jnp.arange(token_count)
    routed = jnp.sum((expert_ids[..., None] == experts).astype(jnp.int32), axis=1)
    before = (tokens[:, None] > tokens[None, :]).astype(bf16)
    slot = jnp.dot(before, routed.astype(bf16), preferred_element_type=f32).astype(jnp.int32)
    selector = (routed[..., None] > 0) & (slot[..., None] == slots)
    selector = selector.reshape(token_count, group_count * capacity).astype(bf16)

    squares = jnp.sum(jnp.square(activations.astype(f32)), axis=1, keepdims=True)
    pieces = [jnp.ones((token_count, 1), bf16)]
    for _ in range(3):
        piece = squares.astype(bf16)
        pieces.append(piece)
        squares = squares - piece.astype(f32)
    extra = jnp.concatenate(
        pieces + [jnp.zeros((token_count, EXTRA - len(pieces)), bf16)], axis=1
    )
    head = jnp.concatenate([activations[:, :LEAD], extra], axis=1)

    def take(chosen, x):
        return lax.dot_general(
            chosen, x, (((0,), (0,)), ((), ())), preferred_element_type=f32
        ).astype(bf16)

    def dispatch(x):
        packed = take(selector, x).reshape(group_count, capacity, x.shape[1])
        out = lax.all_to_all(packed, "expert", split_axis=0, concat_axis=0, tiled=True)
        return out.reshape(group_count * capacity, x.shape[1])

    got_head = dispatch(head)
    got_head, rest = lax.optimization_barrier((got_head, activations[:, LEAD:]))
    got_tail = dispatch(rest)

    h1, p0 = round_one(got_head), both((got_head,))
    h1, p0, got_tail = lax.optimization_barrier((h1, p0, got_tail))
    h2, p1 = lax.optimization_barrier((round_two(*h1), both(h1)))
    h3, p2 = round_three(*h2), both(h2)
    t1, q0 = round_one(got_tail), both((got_tail,))
    h3, p2 = lax.optimization_barrier((h3, p2))
    p3 = both(h3)
    lead = lay_out(p0 + p1 + p2 + p3)

    stats, *factors0 = factor_panel(0, lead)
    (stats, *factors0), t1, q0 = lax.optimization_barrier(((stats, *factors0), t1, q0))
    t2, q1 = round_two(*t1), both(t1)
    factors1 = factor_panel(1, lead, stats, factors0[:2])
    factors1, t2, q1 = lax.optimization_barrier((factors1, t2, q1))
    t3, q2 = round_three(*t2), both(t2)
    partial = own_rows(first_row, lay_out(p0 + p1 + p2), lay_out(q0 + q1 + q2), rows_device)
    partial, t3 = lax.optimization_barrier((partial, t3))
    q3 = both(t3)
    hessian, panels = own_rows(
        first_row,
        lay_out(p3),
        lay_out(q3),
        rows_device,
        (partial, stats, *factors0, *factors1),
    )
    return (hessian[None], panels[None])


def solution(mesh):
    placed = (P(("expert", "tile"), None), P(("expert", "tile"), None))
    return jax.shard_map(
        local,
        mesh=mesh,
        in_specs=placed,
        out_specs=(P("expert", "tile", None), P("expert", "tile", None)),
        check_vma=False,
    )
```

```python
import functools

import jax
import jax.numpy as jnp
from jax import lax
from jax.experimental import pallas as pl
from jax.experimental.pallas import tpu as pltpu
from jax.sharding import PartitionSpec as P

PANEL = 768
LEAD = 2 * PANEL
EXTRA = 128
BLOCK = 256
HALF = 128
MICRO = 8
STRIP = 64
DAMP = 0.01
TILE = 512
WIDTH = 6144

f32 = jnp.float32
bf16 = jnp.bfloat16


def lane_fill(column):
    return jnp.broadcast_to(column, (column.shape[0], HALF))


def row_fill(block, i):
    return jnp.broadcast_to(block[i : i + 1, :], block.shape)


def tree_sum(terms):
    terms = list(terms)
    while len(terms) > 1:
        terms = [
            terms[i] + terms[i + 1] if i + 1 < len(terms) else terms[i]
            for i in range(0, len(terms), 2)
        ]
    return terms[0]


def eliminate(cols, ahead, forward, full_a, full_e, sub):
    roots = None
    for i in range(0, MICRO, 2):
        u, v = cols[i], cols[i + 1]
        p, q, s = row_fill(u, i), row_fill(u, i + 1), row_fill(v, i + 1)
        rd = 1.0 / (p * s - q * q)
        rp = 1.0 / p
        alpha = jnp.where(sub == i + 1, q, u * s - v * q)
        alpha = jnp.where(sub == i, -s, alpha) * rd
        beta = jnp.where(sub == i, q, v * p - u * q)
        beta = jnp.where(sub == i + 1, -p, beta) * rd
        alpha = jnp.where(sub == i, 1.0 + alpha, alpha)
        beta = jnp.where(sub == i + 1, 1.0 + beta, beta)
        below_a = jnp.where(sub > i + 1, alpha, jnp.where(sub == i + 1, q * rp, 0.0))
        below_b = jnp.where(sub > i + 1, beta, 0.0)

        def up(x):
            return x - (alpha * row_fill(x, i) + beta * row_fill(x, i + 1))

        cols = [x if c < i + 2 else up(x) for c, x in enumerate(cols)]
        ahead = [up(x) for x in ahead]
        forward = forward - (below_a * row_fill(forward, i) + below_b * row_fill(forward, i + 1))
        full_a, full_e = up(full_a), up(full_e)
        pair = jnp.where(sub == i, rp, p * rd)
        roots = pair if roots is None else jnp.where(sub >= i, pair, roots)
    return ahead, forward * jnp.sqrt(roots), full_a, full_e


def inverse_factor(read, write, rest_a, rest_e):
    sub = lax.broadcasted_iota(jnp.int32, (MICRO, HALF), 0)
    lane = lax.broadcasted_iota(jnp.int32, (MICRO, HALF), 1)
    unit = lambda g: (lane == sub + MICRO * g).astype(f32)
    groups, width = HALF // MICRO, STRIP // MICRO

    def filled(x, first):
        return [lane_fill(x[:, first + c : first + c + 1]) for c in range(MICRO)]

    for base in range(0, HALF, STRIP):
        final = base + STRIP == HALF
        at = [slice(base + MICRO * g, base + MICRO * (g + 1)) for g in range(width)]
        a = [read(g) if base == 0 else rest_a[at[g], :] for g in range(width)]
        e = [unit(g) if base == 0 else rest_e[at[g], :] for g in range(width)]
        cols = filled(a[0], base)
        for g in range(width):
            first = base + MICRO * g
            more = g + 1 < width
            others = [q for q in range(width) if q != g and not (final and q < g)]
            coef = {q: filled(a[q], first) for q in others}
            ahead = filled(a[g], first + MICRO) if more else []
            following = filled(a[g + 1], first + MICRO) if more else []
            ahead, w, full_a, full_e = eliminate(cols, ahead, e[g], a[g], e[g], sub)
            write(base // MICRO + g, w)
            if more:
                cols = [
                    x - tree_sum([coef[g + 1][i] * row_fill(y, i) for i in range(MICRO)])
                    for x, y in zip(following, ahead)
                ]
            rows_a = [row_fill(full_a, i) for i in range(MICRO)]
            rows_e = [row_fill(full_e, i) for i in range(MICRO)]
            a[g], e[g] = full_a, full_e
            for q in others:
                a[q] = a[q] - tree_sum([coef[q][i] * rows_a[i] for i in range(MICRO)])
                e[q] = e[q] - tree_sum([coef[q][i] * rows_e[i] for i in range(MICRO)])
        if final:
            break
        pad = lambda rows: jnp.concatenate(
            ([jnp.zeros((base, HALF), f32)] if base else [])
            + rows
            + [jnp.zeros((HALF - base - STRIP, HALF), f32)],
            axis=0,
        )
        below = slice(base + STRIP, HALF)
        if base == 0:
            old_a = jnp.concatenate([read(g) for g in range(width, groups)], axis=0)
            old_e = jnp.concatenate([unit(g) for g in range(width, groups)], axis=0)
        else:
            old_a, old_e = rest_a[below, :], rest_e[below, :]
        update = exact(old_a, jnp.concatenate([pad(a), pad(e)], axis=1))
        rest_a[below, :] = old_a - update[:, :HALF]
        rest_e[below, :] = old_e - update[:, HALF:]


def split(x):
    hi = x.astype(bf16)
    return hi, (x - hi.astype(f32)).astype(bf16)


def dot_t(a, b):
    return lax.dot_general(a, b, (((1,), (1,)), ((), ())), preferred_element_type=f32)


def dot3(a, b):
    return dot_t(a[0], b[0]) + (dot_t(a[0], b[1]) + dot_t(a[1], b[0]))


def exact_t(a, b):
    return lax.dot_general(
        a, b, (((1,), (1,)), ((), ())), precision=lax.Precision.HIGHEST, preferred_element_type=f32
    )


def exact(a, b):
    return jnp.dot(a, b, precision=lax.Precision.HIGHEST, preferred_element_type=f32)


def blk(i):
    return pl.ds(pl.multiple_of(i * BLOCK, BLOCK), BLOCK)


def offsets(arrays):
    starts = [0]
    for a in arrays:
        starts.append(starts[-1] + a.shape[0])
    return starts


def gather_columns(pieces, columns, target, sem):
    starts = offsets(pieces)
    copies = [
        pltpu.make_async_copy(
            piece.at[:, columns], target.at[pl.ds(first, piece.shape[0])], sem.at[n]
        )
        for n, (piece, first) in enumerate(zip(pieces, starts))
    ]
    return copies


def cross(a, b):
    return lax.dot_general(a, b, (((0,), (0,)), ((), ())), preferred_element_type=f32)


def panel_kernel(panel, pieces_count, *refs):
    count = PANEL // BLOCK
    pieces = refs[:pieces_count]
    refs = refs[pieces_count:]
    if panel == 0:
        stats, lh, lm, wh, wm, x, sem, col, dd, wd, lower, ra, re = refs
    else:
        stats, eh_all, em_all, lh, lm, wh, wm, x, sem, col, dd, wd, lower, ra, re, eh, em = refs
    first = panel * PANEL
    rows_count = (LEAD - first) // BLOCK
    columns = pl.ds(first, x.shape[1])
    copies = gather_columns(pieces, columns, x, sem)
    if panel == 1:
        below = pl.ds(PANEL, PANEL)
        copies.append(pltpu.make_async_copy(eh_all.at[below], eh, sem.at[len(copies)]))
        copies.append(pltpu.make_async_copy(em_all.at[below], em, sem.at[len(copies)]))
    for c in copies:
        c.start()
    for c in copies:
        c.wait()
    if panel == 0:
        sums = jnp.sum(x[:, LEAD:].astype(f32), axis=0, keepdims=True)
        scale = 2.0 / sums[:, 0:1]
        trace = (sums[:, 1:2] + (sums[:, 2:3] + sums[:, 3:4])) * scale
        damping = DAMP * trace / WIDTH
        stats[0:1, :] = jnp.broadcast_to(scale, (1, EXTRA))
        stats[1:2, :] = jnp.broadcast_to(damping, (1, EXTRA))
        stats[2:8, :] = jnp.zeros((6, EXTRA), f32)
    scale = stats[0:1, 0:1]
    damping = stats[1:2, 0:1]
    eye = (
        lax.broadcasted_iota(jnp.int32, (BLOCK, BLOCK), 0)
        == lax.broadcasted_iota(jnp.int32, (BLOCK, BLOCK), 1)
    ).astype(f32)

    @pl.loop(0, count)
    def _(j):
        @pl.loop(j, rows_count)
        def _(i):
            value = cross(x[:, blk(i)], x[:, blk(j)]) * scale
            if panel == 1:
                value = value - dot3((eh[blk(i), :], em[blk(i), :]), (eh[blk(j), :], em[blk(j), :]))
            col[blk(i), :] = value

            @pl.loop(0, j)
            def _(k):
                col[blk(i), :] -= dot3(
                    (lh[blk(i), blk(k)], lm[blk(i), blk(k)]),
                    (lh[blk(j), blk(k)], lm[blk(j), blk(k)]),
                )

        diag = col[blk(j), :] + damping * eye
        dd[0] = diag[:HALF, :HALF]
        dd[1] = diag[HALF:, HALF:]
        lower[...] = diag[HALF:, :HALF]

        @pl.loop(0, 2)
        def _(s):
            def write(g, value):
                wd[s, g * MICRO : (g + 1) * MICRO, :] = value

            inverse_factor(lambda g: dd[s, g * MICRO : (g + 1) * MICRO, :], write, ra, re)

            @pl.when(s == 0)
            def _():
                lower[...] = exact_t(lower[...], wd[0])
                dd[1] = dd[1] - exact_t(lower[...], lower[...])

        corner = -exact(wd[1], exact(lower[...], wd[0]))
        for piece, value in (
            ((slice(0, HALF), slice(0, HALF)), wd[0]),
            ((slice(HALF, BLOCK), slice(0, HALF)), corner),
            ((slice(HALF, BLOCK), slice(HALF, BLOCK)), wd[1]),
            ((slice(0, HALF), slice(HALF, BLOCK)), jnp.zeros((HALF, HALF), f32)),
        ):
            hi, mid = split(value)
            wh[(j, *piece)] = hi
            wm[(j, *piece)] = mid

        @pl.loop(j + 1, rows_count)
        def _(i):
            hi, mid = split(dot3(split(col[blk(i), :]), (wh[j], wm[j])))
            lh[blk(i), blk(j)] = hi
            lm[blk(i), blk(j)] = mid


def factor_panel(panel, pieces, stats=None, earlier=None):
    rows = LEAD - panel * PANEL
    tokens = sum(p.shape[0] for p in pieces)
    vmem = pl.BlockSpec(memory_space=pltpu.VMEM)
    count = PANEL // BLOCK
    factor = jax.ShapeDtypeStruct((rows, PANEL), bf16)
    inverse = jax.ShapeDtypeStruct((count, BLOCK, BLOCK), bf16)
    out_shape = (factor, factor, inverse, inverse)
    if panel == 0:
        out_shape = (jax.ShapeDtypeStruct((8, EXTRA), f32),) + out_shape
        extra, extra_specs = (), []
    else:
        extra = (stats, *earlier)
        hbm = pl.BlockSpec(memory_space=pl.ANY)
        extra_specs = [vmem, hbm, hbm]
    return pl.pallas_call(
        functools.partial(panel_kernel, panel, len(pieces)),
        out_shape=out_shape,
        in_specs=[pl.BlockSpec(memory_space=pl.ANY)] * len(pieces) + extra_specs,
        out_specs=(vmem,) * len(out_shape),
        scratch_shapes=[
            pltpu.VMEM((tokens, LEAD + EXTRA if panel == 0 else PANEL), bf16),
            pltpu.SemaphoreType.DMA((len(pieces) + 2,)),
            pltpu.VMEM((rows, BLOCK), f32),
            pltpu.VMEM((2, HALF, HALF), f32),
            pltpu.VMEM((2, HALF, HALF), f32),
            pltpu.VMEM((HALF, HALF), f32),
            pltpu.VMEM((HALF, HALF), f32),
            pltpu.VMEM((HALF, HALF), f32),
        ]
        + [pltpu.VMEM((PANEL, PANEL), bf16)] * (2 * panel),
        compiler_params=pltpu.CompilerParams(vmem_limit_bytes=60 << 20),
        cost_estimate=pl.CostEstimate(
            flops=40_000_000_000, bytes_accessed=20_000_000, transcendentals=0
        ),
        name="factor_panel" + str(panel),
    )(*pieces, *extra)


def own_copies(lead, tail, start, rows_device, own, own_sem, act):
    @pl.when(start < LEAD)
    def _():
        at = pl.multiple_of(start, HALF)
        for copy in gather_columns(lead, pl.ds(at, rows_device), own, own_sem):
            act(copy)

    @pl.when(start >= LEAD)
    def _():
        at = pl.multiple_of(start - LEAD, HALF)
        for copy in gather_columns(tail, pl.ds(at, rows_device), own, own_sem):
            act(copy)


def begin(copy):
    copy.start()


def finish(copy):
    copy.wait()


def spot(c):
    return pl.ds(pl.multiple_of(c * TILE, TILE), TILE)


def partial_kernel(n, first_row, *refs):
    lead, tail = refs[:n], refs[n : 2 * n]
    out, own, own_sem, x, x_sem, h, h_sem = refs[2 * n :]
    tiles = WIDTH // TILE
    lead_tiles = LEAD // TILE
    start = pl.multiple_of(first_row[0], HALF)

    def fetch(c, slot, act):
        @pl.when(c < lead_tiles)
        def _():
            for copy in gather_columns(lead, spot(c), x.at[slot], x_sem.at[slot]):
                act(copy)

        @pl.when(jnp.logical_and(c >= lead_tiles, c < tiles))
        def _():
            for copy in gather_columns(tail, spot(c - lead_tiles), x.at[slot], x_sem.at[slot]):
                act(copy)

    own_copies(lead, tail, start, own.shape[1], own, own_sem, begin)
    fetch(0, 0, begin)
    own_copies(lead, tail, start, own.shape[1], own, own_sem, finish)

    def out_copy(c, slot):
        return pltpu.make_async_copy(h.at[slot], out.at[:, spot(c)], h_sem.at[slot])

    @pl.loop(0, tiles)
    def _(c):
        slot = lax.rem(c, 2)
        fetch(c + 1, 1 - slot, begin)
        fetch(c, slot, finish)
        value = cross(own[...], x[slot])

        @pl.when(c >= 2)
        def _():
            out_copy(c - 2, slot).wait()

        h[slot] = value
        out_copy(c, slot).start()

    out_copy(tiles - 2, (tiles - 2) % 2).wait()
    out_copy(tiles - 1, (tiles - 1) % 2).wait()


def final_kernel(n, first_row, *refs):
    lead, tail = refs[:n], refs[n : 2 * n]
    partial, stats = refs[2 * n : 2 * n + 2]
    far = refs[2 * n + 2 : 2 * n + 10]
    hessian, panels = refs[2 * n + 10 : 2 * n + 12]
    own, own_sem, x, x_sem, h, h_sem, o_sem, fh, fm, f_sem = refs[2 * n + 12 : 2 * n + 22]
    near = refs[2 * n + 22 :]
    lh0, lm0, wh0, wm0, lh1, lm1, wh1, wm1 = near
    rows_device = own.shape[1]
    tiles = WIDTH // TILE
    lead_tiles = LEAD // TILE
    start = pl.multiple_of(first_row[0], HALF)
    scale = stats[0:1, 0:1]
    damping = stats[1:2, 0:1]

    def load(c, act):
        pieces, at = (lead, c * TILE) if c < lead_tiles else (tail, (c - lead_tiles) * TILE)
        for copy in gather_columns(pieces, pl.ds(at, TILE), x.at[c], x_sem.at[c]):
            act(copy)
        act(pltpu.make_async_copy(partial.at[:, pl.ds(c * TILE, TILE)], h.at[c], h_sem.at[c]))

    factor_copies = [
        pltpu.make_async_copy(a, b, f_sem.at[k]) for k, (a, b) in enumerate(zip(far, near))
    ]
    own_copies(lead, tail, start, rows_device, own, own_sem, begin)
    for c in range(lead_tiles):
        load(c, begin)
    for copy in factor_copies:
        copy.start()
    for c in range(lead_tiles, tiles):
        load(c, begin)
    own_copies(lead, tail, start, rows_device, own, own_sem, finish)
    row = start + lax.broadcasted_iota(jnp.int32, (rows_device, TILE), 0)
    lane = lax.broadcasted_iota(jnp.int32, (rows_device, TILE), 1)

    def out_copy(c):
        return pltpu.make_async_copy(h.at[c], hessian.at[:, pl.ds(c * TILE, TILE)], o_sem.at[c])

    def tile(c):
        load(c, finish)
        value = (cross(own[...], x[c]) + h[c]) * scale
        h[c] = value + jnp.where(row == lane + c * TILE, damping, 0.0)
        out_copy(c).start()

    for c in range(lead_tiles):
        tile(c)
    for copy in factor_copies:
        copy.wait()
    brow = start + lax.broadcasted_iota(jnp.int32, (rows_device, BLOCK), 0)
    blane = lax.broadcasted_iota(jnp.int32, (rows_device, BLOCK), 1)
    half = PANEL // BLOCK
    for j in range(2 * half):
        here = slice(j * BLOCK, (j + 1) * BLOCK)
        inside = j * BLOCK % TILE
        value = h[j * BLOCK // TILE, :, inside : inside + BLOCK]
        for k in range(j):
            there = slice(k * BLOCK, (k + 1) * BLOCK)
            if k < half:
                rhs = (lh0[here, there], lm0[here, there])
            else:
                a = slice((j - half) * BLOCK, (j - half + 1) * BLOCK)
                b = slice((k - half) * BLOCK, (k - half + 1) * BLOCK)
                rhs = (lh1[a, b], lm1[a, b])
            value = value - dot3((fh[:, there], fm[:, there]), rhs)
        w = (wh0[j], wm0[j]) if j < half else (wh1[j - half], wm1[j - half])
        value = dot3(split(value), w)
        hi, mid = split(value)
        fh[:, here] = hi
        fm[:, here] = mid
        panels[:, here] = jnp.where(brow >= blane + j * BLOCK, value, 0.0)
    for c in range(lead_tiles, tiles):
        tile(c)
    for c in range(tiles):
        out_copy(c).wait()


def own_rows(first_row, lead, tail, rows_device, rest=None):
    tokens = sum(p.shape[0] for p in lead)
    n = len(lead)
    final = rest is not None
    vmem = pl.BlockSpec(memory_space=pltpu.VMEM)
    hbm = pl.BlockSpec(memory_space=pl.ANY)
    block = jax.ShapeDtypeStruct((rows_device, WIDTH), f32)
    dma = pltpu.SemaphoreType.DMA
    depth = WIDTH // TILE if final else 2
    scratch = [
        pltpu.VMEM((tokens, rows_device), bf16),
        dma((n,)),
        pltpu.VMEM((depth, tokens, TILE), bf16),
        dma((depth, n)),
        pltpu.VMEM((depth, rows_device, TILE), f32),
        dma((depth,)),
    ]
    if final:
        scratch += [
            dma((depth,)),
            pltpu.VMEM((rows_device, LEAD), bf16),
            pltpu.VMEM((rows_device, LEAD), bf16),
            dma((8,)),
        ]
        scratch += [pltpu.VMEM(f.shape, f.dtype) for f in rest[2:]]
    specs = [pl.BlockSpec(memory_space=pltpu.SMEM)] + [hbm] * (2 * n)
    return pl.pallas_call(
        functools.partial(final_kernel if final else partial_kernel, n),
        out_shape=(block, jax.ShapeDtypeStruct((rows_device, LEAD), f32)) if final else block,
        in_specs=specs + ([hbm, vmem] + [hbm] * 8 if final else []),
        out_specs=(hbm, vmem) if final else hbm,
        scratch_shapes=scratch,
        compiler_params=pltpu.CompilerParams(vmem_limit_bytes=48 << 20),
        cost_estimate=pl.CostEstimate(
            flops=2 * tokens * rows_device * WIDTH, bytes_accessed=40_000_000, transcendentals=0
        ),
        name="own_rows" + str(int(final)),
    )(first_row.reshape(1), *lead, *tail, *(rest or ()))


UP = [(i, (i + 4) % 16) for i in range(16)]
DOWN = [(i, (i + 12) % 16) for i in range(16)]
ACROSS = [(i, i ^ 2) for i in range(16)]
CORE = [(i, i ^ 1) for i in range(16)]


def move(x, pairs):
    return lax.ppermute(x, "tile", pairs)


def both(blocks):
    return [(b, move(b, CORE)) for b in blocks]


def round_one(b):
    return move(b, UP), move(b, DOWN), move(b, ACROSS)


def round_two(up, down, across):
    return move(up, UP), move(across, DOWN), move(up, ACROSS)


def round_three(up_up, down_across, up_across):
    half = up_across.shape[0] // 2
    return move(up_across[:half], UP), move(down_across[half:], DOWN)


def lay_out(pairs):
    return [a for a, _ in pairs] + [b for _, b in pairs]


def local(activations, expert_ids):
    tile_count = lax.axis_size("tile")
    group_count = lax.axis_size("expert")
    token_count, width = activations.shape
    capacity = 2 * token_count * expert_ids.shape[1] // group_count
    rows_device = width // tile_count
    first_row = lax.axis_index("tile") * rows_device

    experts = jnp.arange(group_count, dtype=jnp.int32)
    slots = jnp.arange(capacity, dtype=jnp.int32)
    tokens = jnp.arange(token_count)
    routed = jnp.sum((expert_ids[..., None] == experts).astype(jnp.int32), axis=1)
    before = (tokens[:, None] > tokens[None, :]).astype(bf16)
    slot = jnp.dot(before, routed.astype(bf16), preferred_element_type=f32).astype(jnp.int32)
    selector = (routed[..., None] > 0) & (slot[..., None] == slots)
    selector = selector.reshape(token_count, group_count * capacity).astype(bf16)

    squares = jnp.sum(jnp.square(activations.astype(f32)), axis=1, keepdims=True)
    pieces = [jnp.ones((token_count, 1), bf16)]
    for _ in range(3):
        piece = squares.astype(bf16)
        pieces.append(piece)
        squares = squares - piece.astype(f32)
    extra = jnp.concatenate(
        pieces + [jnp.zeros((token_count, EXTRA - len(pieces)), bf16)], axis=1
    )
    head = jnp.concatenate([activations[:, :LEAD], extra], axis=1)

    def take(chosen, x):
        return lax.dot_general(
            chosen, x, (((0,), (0,)), ((), ())), preferred_element_type=f32
        ).astype(bf16)

    def pack(x):
        return take(selector, x).reshape(group_count, capacity, x.shape[1])

    def dispatch(packed):
        out = lax.all_to_all(packed, "expert", split_axis=0, concat_axis=0, tiled=True)
        return out.reshape(group_count * capacity, packed.shape[2])

    got_head = dispatch(pack(head))
    packed_tail = pack(activations[:, LEAD:])

    h1, p0 = lax.optimization_barrier((round_one(got_head), both((got_head,))))
    h2, p1, packed_tail = lax.optimization_barrier((round_two(*h1), both(h1), packed_tail))
    got_tail = dispatch(packed_tail)
    h3, p2 = round_three(*h2), both(h2)
    t1, q0 = round_one(got_tail), both((got_tail,))
    h3, p2 = lax.optimization_barrier((h3, p2))
    p3 = both(h3)
    lead = lay_out(p0 + p1 + p2 + p3)

    stats, *factors0 = factor_panel(0, lead)
    (stats, *factors0), t1, q0 = lax.optimization_barrier(((stats, *factors0), t1, q0))
    t2, q1 = round_two(*t1), both(t1)
    factors1 = factor_panel(1, lead, stats, factors0[:2])
    factors1, t2, q1 = lax.optimization_barrier((factors1, t2, q1))
    t3, q2 = round_three(*t2), both(t2)
    early, late = [a for a, _ in p2], [b for _, b in p2]
    partial = own_rows(
        first_row,
        lay_out(p0 + p1) + early,
        lay_out(q0 + q1) + [a for a, _ in q2],
        rows_device,
    )
    partial, t3, q2 = lax.optimization_barrier((partial, t3, q2))
    q3 = both(t3)
    hessian, panels = own_rows(
        first_row,
        late + lay_out(p3),
        [b for _, b in q2] + lay_out(q3),
        rows_device,
        (partial, stats, *factors0, *factors1),
    )
    return (hessian[None], panels[None])


def solution(mesh):
    placed = (P(("expert", "tile"), None), P(("expert", "tile"), None))
    return jax.shard_map(
        local,
        mesh=mesh,
        in_specs=placed,
        out_specs=(P("expert", "tile", None), P("expert", "tile", None)),
        check_vma=False,
    )
```

```python
import functools

import jax
import jax.numpy as jnp
from jax import lax
from jax.experimental import pallas as pl
from jax.experimental.pallas import tpu as pltpu
from jax.sharding import PartitionSpec as P

PANEL = 768
LEAD = 2 * PANEL
EXTRA = 128
BLOCK = 256
HALF = 128
MICRO = 8
STRIP = 64
DAMP = 0.01
TILE = 512
WIDTH = 6144

f32 = jnp.float32
bf16 = jnp.bfloat16


def lane_fill(column):
    return jnp.broadcast_to(column, (column.shape[0], HALF))


def row_fill(block, i):
    return jnp.broadcast_to(block[i : i + 1, :], block.shape)


def tree_sum(terms):
    terms = list(terms)
    while len(terms) > 1:
        terms = [
            terms[i] + terms[i + 1] if i + 1 < len(terms) else terms[i]
            for i in range(0, len(terms), 2)
        ]
    return terms[0]


def eliminate(cols, ahead, rows, sub):
    forward = full = rows
    roots = None
    for i in range(0, MICRO, 2):
        u, v = cols[i], cols[i + 1]
        p, q, s = row_fill(u, i), row_fill(u, i + 1), row_fill(v, i + 1)
        rd = 1.0 / (p * s - q * q)
        rp = 1.0 / p
        alpha = jnp.where(sub == i + 1, q, u * s - v * q)
        alpha = jnp.where(sub == i, -s, alpha) * rd
        beta = jnp.where(sub == i, q, v * p - u * q)
        beta = jnp.where(sub == i + 1, -p, beta) * rd
        alpha = jnp.where(sub == i, 1.0 + alpha, alpha)
        beta = jnp.where(sub == i + 1, 1.0 + beta, beta)
        below_a = jnp.where(sub > i + 1, alpha, jnp.where(sub == i + 1, q * rp, 0.0))
        below_b = jnp.where(sub > i + 1, beta, 0.0)

        def up(x):
            return x - (alpha * row_fill(x, i) + beta * row_fill(x, i + 1))

        cols = [x if c < i + 2 else up(x) for c, x in enumerate(cols)]
        ahead = [up(x) for x in ahead]
        forward = forward - (below_a * row_fill(forward, i) + below_b * row_fill(forward, i + 1))
        full = up(full)
        pair = jnp.where(sub == i, rp, p * rd)
        roots = pair if roots is None else jnp.where(sub >= i, pair, roots)
    return ahead, forward * jnp.sqrt(roots), full


def inverse_factor(read, write, rest):
    sub = lax.broadcasted_iota(jnp.int32, (MICRO, HALF), 0)
    lane = lax.broadcasted_iota(jnp.int32, (MICRO, HALF), 1)
    groups, width = HALF // MICRO, STRIP // MICRO

    def filled(x, first):
        return [lane_fill(x[:, first + c : first + c + 1]) for c in range(MICRO)]

    for base in range(0, HALF, STRIP):
        final = base + STRIP == HALF
        z = [
            read(g) if base == 0 else rest[base + MICRO * g : base + MICRO * (g + 1), :]
            for g in range(width)
        ]
        cols = filled(z[0], base)
        for g in range(width):
            first = base + MICRO * g
            window = (lane >= first) & (lane < first + MICRO)
            unit = (lane == sub + first).astype(f32)
            more = g + 1 < width
            others = [q for q in range(width) if q != g and not (final and q < g)]
            coef = {q: filled(z[q], first) for q in others}
            ahead = filled(z[g], first + MICRO) if more else []
            following = filled(z[g + 1], first + MICRO) if more else []
            ahead, w, z[g] = eliminate(cols, ahead, jnp.where(window, unit, z[g]), sub)
            write(base // MICRO + g, jnp.where(lane < first + MICRO, w, 0.0))
            if more:
                cols = [
                    x - tree_sum([coef[g + 1][i] * row_fill(y, i) for i in range(MICRO)])
                    for x, y in zip(following, ahead)
                ]
            rows = [row_fill(z[g], i) for i in range(MICRO)]
            for q in others:
                z[q] = jnp.where(window, 0.0, z[q]) - tree_sum(
                    [coef[q][i] * rows[i] for i in range(MICRO)]
                )
        if final:
            break
        solved = jnp.concatenate(
            ([jnp.zeros((base, HALF), f32)] if base else [])
            + z
            + [jnp.zeros((HALF - base - STRIP, HALF), f32)],
            axis=0,
        )
        below = slice(base + STRIP, HALF)
        if base == 0:
            old = jnp.concatenate([read(g) for g in range(width, groups)], axis=0)
        else:
            old = rest[below, :]
        column = lax.broadcasted_iota(jnp.int32, old.shape, 1)
        kept = jnp.where((column >= base) & (column < base + STRIP), 0.0, old)
        rest[below, :] = kept - exact(old, solved)


def split(x):
    hi = x.astype(bf16)
    return hi, (x - hi.astype(f32)).astype(bf16)


def dot_t(a, b):
    return lax.dot_general(a, b, (((1,), (1,)), ((), ())), preferred_element_type=f32)


def dot3(a, b):
    return dot_t(a[0], b[0]) + (dot_t(a[0], b[1]) + dot_t(a[1], b[0]))


def exact_t(a, b):
    return lax.dot_general(
        a, b, (((1,), (1,)), ((), ())), precision=lax.Precision.HIGHEST, preferred_element_type=f32
    )


def exact(a, b):
    return jnp.dot(a, b, precision=lax.Precision.HIGHEST, preferred_element_type=f32)


def blk(i):
    return pl.ds(pl.multiple_of(i * BLOCK, BLOCK), BLOCK)


def offsets(arrays):
    starts = [0]
    for a in arrays:
        starts.append(starts[-1] + a.shape[0])
    return starts


def gather_columns(pieces, columns, target, sem):
    starts = offsets(pieces)
    copies = [
        pltpu.make_async_copy(
            piece.at[:, columns], target.at[pl.ds(first, piece.shape[0])], sem.at[n]
        )
        for n, (piece, first) in enumerate(zip(pieces, starts))
    ]
    return copies


def cross(a, b):
    return lax.dot_general(a, b, (((0,), (0,)), ((), ())), preferred_element_type=f32)


def panel_kernel(panel, pieces_count, *refs):
    count = PANEL // BLOCK
    pieces = refs[:pieces_count]
    refs = refs[pieces_count:]
    if panel == 0:
        stats, lh, lm, wh, wm, x, sem, col, dd, wd, lower, ra = refs
    else:
        stats, eh_all, em_all, lh, lm, wh, wm, x, sem, col, dd, wd, lower, ra, eh, em = refs
    first = panel * PANEL
    rows_count = (LEAD - first) // BLOCK

    def block_copies(c):
        here = pl.ds(pl.multiple_of(first + c * BLOCK, BLOCK), BLOCK)
        return gather_columns(pieces, here, x.at[:, blk(c)], sem.at[c])

    once = sem.at[rows_count]
    copies = []
    if panel == 0:
        copies += gather_columns(pieces, pl.ds(LEAD, EXTRA), x.at[:, pl.ds(LEAD, EXTRA)], once)
    if panel == 1:
        below = pl.ds(PANEL, PANEL)
        copies.append(pltpu.make_async_copy(eh_all.at[below], eh, once.at[0]))
        copies.append(pltpu.make_async_copy(em_all.at[below], em, once.at[1]))
    for c in copies:
        c.start()

    @pl.loop(0, rows_count)
    def _(c):
        for copy in block_copies(c):
            copy.start()

    for c in copies:
        c.wait()
    if panel == 0:
        sums = jnp.sum(x[:, LEAD:].astype(f32), axis=0, keepdims=True)
        scale = 2.0 / sums[:, 0:1]
        trace = (sums[:, 1:2] + (sums[:, 2:3] + sums[:, 3:4])) * scale
        damping = DAMP * trace / WIDTH
        stats[0:1, :] = jnp.broadcast_to(scale, (1, EXTRA))
        stats[1:2, :] = jnp.broadcast_to(damping, (1, EXTRA))
        stats[2:8, :] = jnp.zeros((6, EXTRA), f32)
    scale = stats[0:1, 0:1]
    damping = stats[1:2, 0:1]
    eye = (
        lax.broadcasted_iota(jnp.int32, (BLOCK, BLOCK), 0)
        == lax.broadcasted_iota(jnp.int32, (BLOCK, BLOCK), 1)
    ).astype(f32)

    @pl.loop(0, count)
    def _(j):
        @pl.loop(j, rows_count)
        def _(i):
            @pl.when(j == 0)
            def _():
                for copy in block_copies(i):
                    copy.wait()

            value = cross(x[:, blk(i)], x[:, blk(j)]) * scale
            if panel == 1:
                value = value - dot3((eh[blk(i), :], em[blk(i), :]), (eh[blk(j), :], em[blk(j), :]))
            col[blk(i), :] = value

            @pl.loop(0, j)
            def _(k):
                col[blk(i), :] -= dot3(
                    (lh[blk(i), blk(k)], lm[blk(i), blk(k)]),
                    (lh[blk(j), blk(k)], lm[blk(j), blk(k)]),
                )

        diag = col[blk(j), :] + damping * eye
        dd[0] = diag[:HALF, :HALF]
        dd[1] = diag[HALF:, HALF:]
        lower[...] = diag[HALF:, :HALF]

        @pl.loop(0, 2)
        def _(s):
            def write(g, value):
                wd[s, g * MICRO : (g + 1) * MICRO, :] = value

            inverse_factor(lambda g: dd[s, g * MICRO : (g + 1) * MICRO, :], write, ra)

            @pl.when(s == 0)
            def _():
                lower[...] = exact_t(lower[...], wd[0])
                dd[1] = dd[1] - exact_t(lower[...], lower[...])

        corner = -exact(wd[1], exact(lower[...], wd[0]))
        for piece, value in (
            ((slice(0, HALF), slice(0, HALF)), wd[0]),
            ((slice(HALF, BLOCK), slice(0, HALF)), corner),
            ((slice(HALF, BLOCK), slice(HALF, BLOCK)), wd[1]),
            ((slice(0, HALF), slice(HALF, BLOCK)), jnp.zeros((HALF, HALF), f32)),
        ):
            hi, mid = split(value)
            wh[(j, *piece)] = hi
            wm[(j, *piece)] = mid

        @pl.loop(j + 1, rows_count)
        def _(i):
            hi, mid = split(dot3(split(col[blk(i), :]), (wh[j], wm[j])))
            lh[blk(i), blk(j)] = hi
            lm[blk(i), blk(j)] = mid


def factor_panel(panel, pieces, stats=None, earlier=None):
    rows = LEAD - panel * PANEL
    tokens = sum(p.shape[0] for p in pieces)
    vmem = pl.BlockSpec(memory_space=pltpu.VMEM)
    count = PANEL // BLOCK
    factor = jax.ShapeDtypeStruct((rows, PANEL), bf16)
    inverse = jax.ShapeDtypeStruct((count, BLOCK, BLOCK), bf16)
    out_shape = (factor, factor, inverse, inverse)
    if panel == 0:
        out_shape = (jax.ShapeDtypeStruct((8, EXTRA), f32),) + out_shape
        extra, extra_specs = (), []
    else:
        extra = (stats, *earlier)
        hbm = pl.BlockSpec(memory_space=pl.ANY)
        extra_specs = [vmem, hbm, hbm]
    return pl.pallas_call(
        functools.partial(panel_kernel, panel, len(pieces)),
        out_shape=out_shape,
        in_specs=[pl.BlockSpec(memory_space=pl.ANY)] * len(pieces) + extra_specs,
        out_specs=(vmem,) * len(out_shape),
        scratch_shapes=[
            pltpu.VMEM((tokens, LEAD + EXTRA if panel == 0 else PANEL), bf16),
            pltpu.SemaphoreType.DMA((rows // BLOCK + 1, len(pieces))),
            pltpu.VMEM((rows, BLOCK), f32),
            pltpu.VMEM((2, HALF, HALF), f32),
            pltpu.VMEM((2, HALF, HALF), f32),
            pltpu.VMEM((HALF, HALF), f32),
            pltpu.VMEM((HALF, HALF), f32),
        ]
        + [pltpu.VMEM((PANEL, PANEL), bf16)] * (2 * panel),
        compiler_params=pltpu.CompilerParams(vmem_limit_bytes=60 << 20),
        cost_estimate=pl.CostEstimate(
            flops=40_000_000_000, bytes_accessed=20_000_000, transcendentals=0
        ),
        name="factor_panel" + str(panel),
    )(*pieces, *extra)


def own_copies(lead, tail, start, rows_device, own, own_sem, act):
    @pl.when(start < LEAD)
    def _():
        at = pl.multiple_of(start, HALF)
        for copy in gather_columns(lead, pl.ds(at, rows_device), own, own_sem):
            act(copy)

    @pl.when(start >= LEAD)
    def _():
        at = pl.multiple_of(start - LEAD, HALF)
        for copy in gather_columns(tail, pl.ds(at, rows_device), own, own_sem):
            act(copy)


def begin(copy):
    copy.start()


def finish(copy):
    copy.wait()


def spot(c):
    return pl.ds(pl.multiple_of(c * TILE, TILE), TILE)


def partial_kernel(n, first_row, *refs):
    lead, tail = refs[:n], refs[n : 2 * n]
    out, own, own_sem, x, x_sem, h, h_sem = refs[2 * n :]
    tiles = WIDTH // TILE
    lead_tiles = LEAD // TILE
    start = pl.multiple_of(first_row[0], HALF)

    def fetch(c, slot, act):
        @pl.when(c < lead_tiles)
        def _():
            for copy in gather_columns(lead, spot(c), x.at[slot], x_sem.at[slot]):
                act(copy)

        @pl.when(jnp.logical_and(c >= lead_tiles, c < tiles))
        def _():
            for copy in gather_columns(tail, spot(c - lead_tiles), x.at[slot], x_sem.at[slot]):
                act(copy)

    own_copies(lead, tail, start, own.shape[1], own, own_sem, begin)
    fetch(0, 0, begin)
    own_copies(lead, tail, start, own.shape[1], own, own_sem, finish)

    def out_copy(c, slot):
        return pltpu.make_async_copy(h.at[slot], out.at[:, spot(c)], h_sem.at[slot])

    @pl.loop(0, tiles)
    def _(c):
        slot = lax.rem(c, 2)
        fetch(c + 1, 1 - slot, begin)
        fetch(c, slot, finish)
        value = cross(own[...], x[slot])

        @pl.when(c >= 2)
        def _():
            out_copy(c - 2, slot).wait()

        h[slot] = value
        out_copy(c, slot).start()

    out_copy(tiles - 2, (tiles - 2) % 2).wait()
    out_copy(tiles - 1, (tiles - 1) % 2).wait()


def final_kernel(n, first_row, *refs):
    lead, tail = refs[:n], refs[n : 2 * n]
    partial, stats = refs[2 * n : 2 * n + 2]
    far = refs[2 * n + 2 : 2 * n + 10]
    hessian, panels = refs[2 * n + 10 : 2 * n + 12]
    own, own_sem, x, x_sem, h, h_sem, o_sem, fh, fm, f_sem = refs[2 * n + 12 : 2 * n + 22]
    near = refs[2 * n + 22 :]
    lh0, lm0, wh0, wm0, lh1, lm1, wh1, wm1 = near
    rows_device = own.shape[1]
    tiles = WIDTH // TILE
    lead_tiles = LEAD // TILE
    start = pl.multiple_of(first_row[0], HALF)
    scale = stats[0:1, 0:1]
    damping = stats[1:2, 0:1]

    def load(c, act):
        pieces, at = (lead, c * TILE) if c < lead_tiles else (tail, (c - lead_tiles) * TILE)
        for copy in gather_columns(pieces, pl.ds(at, TILE), x.at[c], x_sem.at[c]):
            act(copy)
        act(pltpu.make_async_copy(partial.at[:, pl.ds(c * TILE, TILE)], h.at[c], h_sem.at[c]))

    factor_copies = [
        pltpu.make_async_copy(a, b, f_sem.at[k]) for k, (a, b) in enumerate(zip(far, near))
    ]
    own_copies(lead, tail, start, rows_device, own, own_sem, begin)
    for c in range(lead_tiles):
        load(c, begin)
    for copy in factor_copies:
        copy.start()
    for c in range(lead_tiles, tiles):
        load(c, begin)
    own_copies(lead, tail, start, rows_device, own, own_sem, finish)
    row = start + lax.broadcasted_iota(jnp.int32, (rows_device, TILE), 0)
    lane = lax.broadcasted_iota(jnp.int32, (rows_device, TILE), 1)

    def out_copy(c):
        return pltpu.make_async_copy(h.at[c], hessian.at[:, pl.ds(c * TILE, TILE)], o_sem.at[c])

    def tile(c):
        load(c, finish)
        value = (cross(own[...], x[c]) + h[c]) * scale
        h[c] = value + jnp.where(row == lane + c * TILE, damping, 0.0)
        out_copy(c).start()

    for c in range(lead_tiles):
        tile(c)
    for copy in factor_copies:
        copy.wait()
    brow = start + lax.broadcasted_iota(jnp.int32, (rows_device, BLOCK), 0)
    blane = lax.broadcasted_iota(jnp.int32, (rows_device, BLOCK), 1)
    half = PANEL // BLOCK
    for j in range(2 * half):
        here = slice(j * BLOCK, (j + 1) * BLOCK)
        inside = j * BLOCK % TILE
        value = h[j * BLOCK // TILE, :, inside : inside + BLOCK]
        for k in range(j):
            there = slice(k * BLOCK, (k + 1) * BLOCK)
            if k < half:
                rhs = (lh0[here, there], lm0[here, there])
            else:
                a = slice((j - half) * BLOCK, (j - half + 1) * BLOCK)
                b = slice((k - half) * BLOCK, (k - half + 1) * BLOCK)
                rhs = (lh1[a, b], lm1[a, b])
            value = value - dot3((fh[:, there], fm[:, there]), rhs)
        w = (wh0[j], wm0[j]) if j < half else (wh1[j - half], wm1[j - half])
        value = dot3(split(value), w)
        hi, mid = split(value)
        fh[:, here] = hi
        fm[:, here] = mid
        panels[:, here] = jnp.where(brow >= blane + j * BLOCK, value, 0.0)
    for c in range(lead_tiles, tiles):
        tile(c)
    for c in range(tiles):
        out_copy(c).wait()


def own_rows(first_row, lead, tail, rows_device, rest=None):
    tokens = sum(p.shape[0] for p in lead)
    n = len(lead)
    final = rest is not None
    vmem = pl.BlockSpec(memory_space=pltpu.VMEM)
    hbm = pl.BlockSpec(memory_space=pl.ANY)
    block = jax.ShapeDtypeStruct((rows_device, WIDTH), f32)
    dma = pltpu.SemaphoreType.DMA
    depth = WIDTH // TILE if final else 2
    scratch = [
        pltpu.VMEM((tokens, rows_device), bf16),
        dma((n,)),
        pltpu.VMEM((depth, tokens, TILE), bf16),
        dma((depth, n)),
        pltpu.VMEM((depth, rows_device, TILE), f32),
        dma((depth,)),
    ]
    if final:
        scratch += [
            dma((depth,)),
            pltpu.VMEM((rows_device, LEAD), bf16),
            pltpu.VMEM((rows_device, LEAD), bf16),
            dma((8,)),
        ]
        scratch += [pltpu.VMEM(f.shape, f.dtype) for f in rest[2:]]
    specs = [pl.BlockSpec(memory_space=pltpu.SMEM)] + [hbm] * (2 * n)
    return pl.pallas_call(
        functools.partial(final_kernel if final else partial_kernel, n),
        out_shape=(block, jax.ShapeDtypeStruct((rows_device, LEAD), f32)) if final else block,
        in_specs=specs + ([hbm, vmem] + [hbm] * 8 if final else []),
        out_specs=(hbm, vmem) if final else hbm,
        scratch_shapes=scratch,
        compiler_params=pltpu.CompilerParams(vmem_limit_bytes=48 << 20),
        cost_estimate=pl.CostEstimate(
            flops=2 * tokens * rows_device * WIDTH, bytes_accessed=40_000_000, transcendentals=0
        ),
        name="own_rows" + str(int(final)),
    )(first_row.reshape(1), *lead, *tail, *(rest or ()))


UP = [(i, (i + 4) % 16) for i in range(16)]
DOWN = [(i, (i + 12) % 16) for i in range(16)]
ACROSS = [(i, i ^ 2) for i in range(16)]
CORE = [(i, i ^ 1) for i in range(16)]


def move(x, pairs):
    return lax.ppermute(x, "tile", pairs)


def both(blocks):
    return [(b, move(b, CORE)) for b in blocks]


def round_one(b):
    return move(b, UP), move(b, DOWN), move(b, ACROSS)


def round_two(up, down, across):
    return move(up, UP), move(across, DOWN), move(up, ACROSS)


def round_three(up_up, down_across, up_across):
    half = up_across.shape[0] // 2
    return move(up_across[:half], UP), move(down_across[half:], DOWN)


def lay_out(pairs):
    return [a for a, _ in pairs] + [b for _, b in pairs]


def local(activations, expert_ids):
    tile_count = lax.axis_size("tile")
    group_count = lax.axis_size("expert")
    token_count, width = activations.shape
    capacity = 2 * token_count * expert_ids.shape[1] // group_count
    rows_device = width // tile_count
    first_row = lax.axis_index("tile") * rows_device

    experts = jnp.arange(group_count, dtype=jnp.int32)
    slots = jnp.arange(capacity, dtype=jnp.int32)
    tokens = jnp.arange(token_count)
    routed = jnp.sum((expert_ids[..., None] == experts).astype(jnp.int32), axis=1)
    before = (tokens[:, None] > tokens[None, :]).astype(bf16)
    slot = jnp.dot(before, routed.astype(bf16), preferred_element_type=f32).astype(jnp.int32)
    selector = (routed[..., None] > 0) & (slot[..., None] == slots)
    selector = selector.reshape(token_count, group_count * capacity).astype(bf16)

    squares = jnp.sum(jnp.square(activations.astype(f32)), axis=1, keepdims=True)
    pieces = [jnp.ones((token_count, 1), bf16)]
    for _ in range(3):
        piece = squares.astype(bf16)
        pieces.append(piece)
        squares = squares - piece.astype(f32)
    extra = jnp.concatenate(
        pieces + [jnp.zeros((token_count, EXTRA - len(pieces)), bf16)], axis=1
    )
    head = jnp.concatenate([activations[:, :LEAD], extra], axis=1)

    def take(chosen, x):
        return lax.dot_general(
            chosen, x, (((0,), (0,)), ((), ())), preferred_element_type=f32
        ).astype(bf16)

    def pack(x):
        return take(selector, x).reshape(group_count, capacity, x.shape[1])

    def dispatch(packed):
        out = lax.all_to_all(packed, "expert", split_axis=0, concat_axis=0, tiled=True)
        return out.reshape(group_count * capacity, packed.shape[2])

    got_head = dispatch(pack(head))
    packed_tail = pack(activations[:, LEAD:])

    h1, p0 = lax.optimization_barrier((round_one(got_head), both((got_head,))))
    h2, p1, packed_tail = lax.optimization_barrier((round_two(*h1), both(h1), packed_tail))
    got_tail = dispatch(packed_tail)
    h3, p2 = round_three(*h2), both(h2)
    t1, q0 = round_one(got_tail), both((got_tail,))
    h3, p2 = lax.optimization_barrier((h3, p2))
    p3 = both(h3)
    lead = lay_out(p0 + p1 + p2 + p3)

    stats, *factors0 = factor_panel(0, lead)
    (stats, *factors0), t1, q0 = lax.optimization_barrier(((stats, *factors0), t1, q0))
    t2, q1 = round_two(*t1), both(t1)
    factors1 = factor_panel(1, lead, stats, factors0[:2])
    factors1, t2, q1 = lax.optimization_barrier((factors1, t2, q1))
    t3, q2 = round_three(*t2), both(t2)
    early, late = [a for a, _ in p2], [b for _, b in p2]
    partial = own_rows(
        first_row,
        lay_out(p0 + p1) + early,
        lay_out(q0 + q1) + [a for a, _ in q2],
        rows_device,
    )
    partial, t3, q2 = lax.optimization_barrier((partial, t3, q2))
    q3 = both(t3)
    hessian, panels = own_rows(
        first_row,
        late + lay_out(p3),
        [b for _, b in q2] + lay_out(q3),
        rows_device,
        (partial, stats, *factors0, *factors1),
    )
    return (hessian[None], panels[None])


def solution(mesh):
    placed = (P(("expert", "tile"), None), P(("expert", "tile"), None))
    return jax.shard_map(
        local,
        mesh=mesh,
        in_specs=placed,
        out_specs=(P("expert", "tile", None), P("expert", "tile", None)),
        check_vma=False,
    )
```
